1024 devices in a mesh: ep: 16 (over x_hi, y, core), dp: 64 (over x_lo, z).
Axes of the slice: x: 4 (x_hi: 2, x_lo: 2; x = x_hi * 2 + x_lo), y: 4, z: 32, core: 2. Of those that a mesh axis runs over, the one named last changes fastest.
Arguments:
- fwd_tokens: bfloat16 [16384, 2048], P(('ep', 'dp')), may hold values from -6 to 6
- fwd_routes: int32 [16384, 8], P(('ep', 'dp')), may hold values from 0 to 15, as said below
- fwd_weights: float32 [16384, 8], P(('ep', 'dp')), may hold values from 0.05 to 0.4
- bwd_grads: bfloat16 [16384, 2048], P(('ep', 'dp')), may hold values from -24 to 24
- bwd_routes: int32 [16384, 8], P(('ep', 'dp')), may hold values from 0 to 15, as said below
- bwd_weights: float32 [16384, 8], P(('ep', 'dp')), may hold values from 0.05 to 0.4
- bwd_saved: bfloat16 [16, 8192, 2048], P('ep', 'dp'), may hold values from -6 to 6
- w_gate: bfloat16 [16, 2048, 384], P('ep'), may hold values from -0.125 to 0.125
- w_up: bfloat16 [16, 2048, 384], P('ep'), may hold values from -0.125 to 0.125
- w_down: bfloat16 [16, 384, 2048], P('ep'), may hold values from -0.3125 to 0.3125
Outputs:
- fwd_out: bfloat16 [16384, 2048], P(('ep', 'dp'))
- bwd_input_grad: bfloat16 [16384, 2048], P(('ep', 'dp'))
- down_grad: float32 [16, 2048, 384], P('ep', 'dp')
The draws below stay inside these ranges and needn't reach their ends.
Inputs may be any that keep to these rules, and one draw needn't show every extreme that they name: `fwd_routes`: each token names 8 different experts, and the 16 tokens of each aligned block (one device's tokens) name every expert exactly 8 times. `bwd_routes`: each token names 8 different experts, and the 16 tokens of each aligned block (one device's tokens) name every expert exactly 8 times.
All inputs are finite; a program needn't handle non-finite values.
Results may differ from the reference program's by a relative error of at most 0.0064.
Values may be sent and summed in bfloat16 or wider, within the bound.
No kernel may reach another device: no remote copies, remote signals or barrier semaphores. Data moves between devices by JAX's collectives and lax.ppermute only.
A program may use at most 32 MiB of HBM per device.

```python
import math
import jax
import jax.numpy as jnp
from jax import lax

D = 2048
FF = 384
TOK = 16
EXPERTS = 16
TOP = 8
TOKENS = 16384
ROWS = 8192
N_EP = 16
N_DP = 64


def route_group(key):
    first, second, third = jax.random.split(key, 3)
    expert_perm = jax.random.permutation(first, EXPERTS)
    offsets = jax.random.permutation(second, EXPERTS)[:TOP]
    shuffle = jax.random.permutation(third, EXPERTS)
    position = (shuffle[:, None] + offsets[None, :]) % EXPERTS
    return expert_perm[position]


def route_block(key):
    keys_all = jax.random.split(key, TOK // EXPERTS + 1)
    grouped = jax.vmap(route_group)(keys_all[1:]).reshape(TOK, TOP)
    reorder = jax.random.permutation(keys_all[0], TOK)
    return grouped[reorder]


def route_table(key):
    keys_all = jax.random.split(key, TOKENS // TOK)
    return jax.vmap(route_block)(keys_all).reshape(TOKENS, TOP).astype(jnp.int32)


def draw_fwd_routes(key, part):
    return route_table(jax.random.fold_in(key, 11))


def draw_bwd_routes(key, part):
    return route_table(jax.random.fold_in(key, 23))


def raised(array, rng, source, target, shards_of, factor):
    def block_of(dim):
        return (jnp.arange(array.shape[dim]) // (array.shape[dim] // shards_of)).reshape((-1,) + (1,) * (array.ndim - 1 - dim))

    one_side = jax.random.permutation(rng, shards_of)[block_of(target)]
    far = (block_of(target) + shards_of // 2) % shards_of
    return jnp.where((block_of(source) == one_side) | (block_of(source) == far), factor * array, array)


def level_of(key, shape, cuts, smallest, top_value):
    gain, own = 1.0, jax.random.fold_in(key, 6)
    for dim, parts in cuts:
        steps = jnp.exp(jax.random.uniform(jax.random.fold_in(own, dim), (parts,), jnp.float32, smallest / len(cuts), top_value / len(cuts)))
        gain = gain * jnp.repeat(steps, shape[dim] // parts).reshape([-1 if axis == dim else 1 for axis in range(len(shape))])
    return gain


def bell_draw(key, shape, deviation, limit, pieces=(), kind=jnp.bfloat16):
    level = level_of(key, shape, pieces, -0.22, 0.18) if pieces else 1.0
    drawn = jax.random.normal(key, shape, jnp.float32) * deviation * level
    return jnp.minimum(jnp.maximum(drawn, -limit), limit).astype(kind)


def gaussian_with(stream_key, dims, spread, bound, shards, heavy, kind=jnp.bfloat16):
    entries = spread * jax.random.normal(stream_key, dims, jnp.float32)
    if shards:
        entries = entries * level_of(stream_key, dims, shards, -0.22, 0.18)
    return jnp.clip(raised(entries, jax.random.fold_in(stream_key, 3), *heavy), -bound, bound).astype(kind)


def setup_inputs(seed: int = 0) -> dict:
    key_of = jax.random.split(jax.random.key(seed), 11)
    fwd_tokens = bell_draw(key_of[0], (TOKENS, D), 1.0, 6.0, ((0, 1024),))
    fwd_routes = draw_fwd_routes(jax.random.fold_in(key_of[10], 71), 0)
    fwd_weights = jnp.clip(jnp.exp(math.log(0.4) - 2.0794415 * jax.random.uniform(key_of[2], (TOKENS, TOP), jnp.float32) ** level_of(key_of[2], (TOKENS, TOP), ((0, 1024),), -0.2, 0.2)), 0.05, 0.4)
    bwd_grads = gaussian_with(key_of[3], (TOKENS, D), 1.0, 24.0, ((0, 1024),), (0, 1, 1024, 6.0))
    bwd_routes = draw_bwd_routes(jax.random.fold_in(key_of[10], 71), 0)
    bwd_weights = jnp.clip(jnp.exp(math.log(0.4) - 2.0794415 * jax.random.uniform(key_of[5], (TOKENS, TOP), jnp.float32) ** level_of(key_of[5], (TOKENS, TOP), ((0, 1024),), -0.2, 0.2)), 0.05, 0.4)
    bwd_saved = bell_draw(key_of[6], (EXPERTS, ROWS, D), 1.0, 6.0, ((0, 16), (1, 64)))
    w_gate = bell_draw(key_of[7], (EXPERTS, D, FF), D ** -0.5, 0.125, ((0, 16),))
    w_up = bell_draw(key_of[8], (EXPERTS, D, FF), D ** -0.5, 0.125, ((0, 16),))
    w_down = bell_draw(key_of[9], (EXPERTS, FF, D), FF ** -0.5, 0.3125, ((0, 16),))
    return {"fwd_tokens": fwd_tokens, "fwd_routes": fwd_routes, "fwd_weights": fwd_weights, "bwd_grads": bwd_grads, "bwd_routes": bwd_routes, "bwd_weights": bwd_weights, "bwd_saved": bwd_saved, "w_gate": w_gate, "w_up": w_up, "w_down": w_down}


def slot_order(routes):
    blocks = routes.shape[0] // TOK
    block_of = jnp.arange(routes.shape[0], dtype=jnp.int32) // TOK
    source = (block_of % N_DP) * N_EP + block_of // N_DP
    sort_keys = routes * blocks + source[:, None]
    ranked = jnp.argsort(sort_keys.reshape(-1), stable=True).astype(jnp.int32)
    return ranked.reshape(EXPERTS, -1)


def reference(fwd_tokens, fwd_routes, fwd_weights, bwd_grads, bwd_routes, bwd_weights, bwd_saved, w_gate, w_up, w_down):
    fwd_slots = slot_order(fwd_routes)
    fwd_flat = fwd_weights.reshape(-1)
    bwd_slots = slot_order(bwd_routes)
    bwd_flat = bwd_weights.reshape(-1)
    contract_last = (((1,), (1,)), ((), ()))
    contract_rows = (((0,), (0,)), ((), ()))

    def forward_step(summed, inputs):
        picked, gate_w, up_w, down_w = inputs
        token_ids = picked // TOP
        expert_in = fwd_tokens[token_ids]
        gate_pre = jnp.dot(expert_in, gate_w, preferred_element_type=jnp.float32)
        up_pre = jnp.dot(expert_in, up_w, preferred_element_type=jnp.float32)
        hidden = (jax.nn.silu(gate_pre) * up_pre).astype(jnp.bfloat16)
        expert_out = jnp.dot(hidden, down_w, preferred_element_type=jnp.float32).astype(jnp.bfloat16)
        summed = summed.at[token_ids].add(fwd_flat[picked][:, None] * expert_out.astype(jnp.float32))
        return summed, None

    fwd_sum, unused = lax.scan(forward_step, jnp.zeros(fwd_tokens.shape, jnp.float32), (fwd_slots, w_gate, w_up, w_down))

    def backward_step(summed, inputs):
        picked, saved_rows, gate_w, up_w, down_w = inputs
        token_ids = picked // TOP
        cot_rows = (bwd_flat[picked][:, None] * bwd_grads[token_ids].astype(jnp.float32)).astype(jnp.bfloat16)
        gate_pre = jnp.dot(saved_rows, gate_w, preferred_element_type=jnp.float32)
        up_pre = jnp.dot(saved_rows, up_w, preferred_element_type=jnp.float32)
        sigma = jax.nn.sigmoid(gate_pre)
        hidden = (gate_pre * sigma * up_pre).astype(jnp.bfloat16)
        dact = lax.dot_general(cot_rows, down_w, contract_last, preferred_element_type=jnp.float32)
        dgate = (dact * up_pre * sigma * (1.0 + gate_pre * (1.0 - sigma))).astype(jnp.bfloat16)
        dup_rows = (dact * gate_pre * sigma).astype(jnp.bfloat16)
        row_grad = lax.dot_general(dgate, gate_w, contract_last, preferred_element_type=jnp.float32)
        row_grad = (row_grad + lax.dot_general(dup_rows, up_w, contract_last, preferred_element_type=jnp.float32)).astype(jnp.bfloat16)
        summed = summed.at[token_ids].add(row_grad.astype(jnp.float32))
        weight_term = lax.dot_general(cot_rows, hidden, contract_rows, preferred_element_type=jnp.float32)
        return summed, weight_term

    bwd_sum, down_grad = lax.scan(backward_step, jnp.zeros(bwd_grads.shape, jnp.float32), (bwd_slots, bwd_saved, w_gate, w_up, w_down))
    return fwd_sum.astype(jnp.bfloat16), bwd_sum.astype(jnp.bfloat16), down_grad
```

```python
import jax
import jax.numpy as jnp
from jax import lax
from jax.experimental import pallas as pl
from jax.experimental.pallas import tpu as pltpu
from jax.sharding import PartitionSpec as P

EXPERTS = 16
SLOTS = 8
NEAR = 4
BF16, F32 = jnp.bfloat16, jnp.float32


def slot_matrix(routes_t, weights_t):
    picks, tokens = routes_t.shape
    rows = EXPERTS * SLOTS
    row = lax.broadcasted_iota(jnp.int32, (rows, tokens), 0)
    expert, slot = row // SLOTS, row % SLOTS
    member = jnp.zeros((rows, tokens), F32)
    mixing = jnp.zeros((rows, tokens), F32)
    for k in range(picks):
        hit = routes_t[k : k + 1, :] == expert
        member = member + jnp.where(hit, 1.0, 0.0)
        mixing = mixing + jnp.where(hit, weights_t[k : k + 1, :], 0.0)
    earlier = lax.broadcasted_iota(jnp.int32, (tokens, tokens), 0) < lax.broadcasted_iota(
        jnp.int32, (tokens, tokens), 1
    )
    before = jnp.dot(
        member.astype(BF16), jnp.where(earlier, 1.0, 0.0).astype(BF16), preferred_element_type=F32
    )
    chosen = (member > 0.5) & (before.astype(jnp.int32) == slot)
    return jnp.where(chosen, 1.0, 0.0), jnp.where(chosen, mixing, 0.0)


def select_kernel(scaled, routes_ref, weights_ref, x_ref, out_ref):
    chosen, mixing = slot_matrix(routes_ref[...], weights_ref[...])
    scale = jnp.sum(mixing, axis=1, keepdims=True)
    chosen = chosen.astype(BF16)
    for c in range(0, x_ref.shape[1], 256):
        rows = jnp.dot(chosen, x_ref[:, c : c + 256], preferred_element_type=F32)
        if scaled:
            rows = rows * scale
        out_ref[:, c : c + 256] = rows.astype(BF16)


def select(routes, weights, x, scaled):
    import functools

    rows, width = EXPERTS * SLOTS, x.shape[1]
    return pl.pallas_call(
        functools.partial(select_kernel, scaled),
        out_shape=jax.ShapeDtypeStruct((rows, width), BF16),
        cost_estimate=pl.CostEstimate(flops=2 * rows * 16 * width, bytes_accessed=rows * width * 4, transcendentals=0),
        name="select_scaled" if scaled else "select_plain",
    )(routes.T, weights.T, x)


def combine_kernel(weighted, routes_ref, weights_ref, rows_ref, out_ref):
    chosen, mixing = slot_matrix(routes_ref[...], weights_ref[...])
    contract_rows = (((0,), (0,)), ((), ()))
    if weighted:
        high = mixing.astype(BF16)
        rest = mixing - high.astype(F32)
        middle = rest.astype(BF16)
        low = (rest - middle.astype(F32)).astype(BF16)
        parts = [low, middle, high]
    else:
        parts = [chosen.astype(BF16)]
    parts = [p.astype(F32).T.astype(BF16) for p in parts]
    for c in range(0, rows_ref.shape[1], 512):
        rows = rows_ref[:, c : c + 512]
        total = jnp.dot(parts[0], rows, preferred_element_type=F32)
        for p in parts[1:]:
            total = total + jnp.dot(p, rows, preferred_element_type=F32)
        out_ref[:, c : c + 512] = total.astype(BF16)


def combine(routes, weights, rows, weighted):
    import functools

    return pl.pallas_call(
        functools.partial(combine_kernel, weighted),
        out_shape=jax.ShapeDtypeStruct((routes.shape[0], rows.shape[1]), BF16),
        cost_estimate=pl.CostEstimate(flops=10**7, bytes_accessed=rows.size * 2, transcendentals=0),
        name="combine_weighted" if weighted else "combine_plain",
    )(routes.T, weights.T, rows)


def split_kernel(cot_ref, out_ref):
    members, columns, rows = out_ref.shape
    halves = members // NEAR
    fars = cot_ref.shape[1] // (halves * 128)
    sub = 128 // NEAR
    for half in range(halves):
        for far in range(fars):
            at = (half * fars + far) * 128
            tile = cot_ref[:, at : at + 128].astype(F32).T.astype(BF16)
            for k in range(NEAR):
                out_ref[half * NEAR + k, far * sub : (far + 1) * sub, :] = tile[k * sub : (k + 1) * sub, :]


def split_columns(cot, members):
    rows, width = cot.shape
    return pl.pallas_call(
        split_kernel,
        out_shape=jax.ShapeDtypeStruct((members, width // members, rows), BF16),
        cost_estimate=pl.CostEstimate(flops=10**6, bytes_accessed=rows * width * 4, transcendentals=0),
        name="split_columns",
    )(cot)


def grad_kernel(cot_ref, act_ref, out_ref):
    total = jnp.zeros(out_ref.shape, F32)
    for s in range(cot_ref.shape[0]):
        total = total + jnp.dot(cot_ref[s], act_ref[s], preferred_element_type=F32)
    out_ref[...] = total.astype(BF16)


def grad_part(cot_t, act):
    members, columns, rows = cot_t.shape
    return pl.pallas_call(
        grad_kernel,
        out_shape=jax.ShapeDtypeStruct((columns, act.shape[2]), BF16),
        cost_estimate=pl.CostEstimate(
            flops=2 * members * columns * rows * act.shape[2], bytes_accessed=cot_t.size * 4, transcendentals=0
        ),
        name="grad_part",
    )(cot_t, act)


def on_device(
    fwd_tokens, fwd_routes, fwd_weights, bwd_grads, bwd_routes, bwd_weights, bwd_saved, w_gate, w_up, w_down
):
    dp = lax.axis_size("dp")
    depth = dp // 2
    fars = depth // NEAR
    near = [[x * depth + f * NEAR + k for x in range(2) for k in range(NEAR)] for f in range(fars)]
    far = [[x * depth + f * NEAR + k for f in range(fars)] for x in range(2) for k in range(NEAR)]
    width = fwd_tokens.shape[1]
    rows = EXPERTS * SLOTS
    contract_last = (((1,), (1,)), ((), ()))
    gate_w, up_w, down_w = w_gate[0], w_up[0], w_down[0]

    def swap(x, axis="ep", groups=None):
        return lax.all_to_all(x, axis, split_axis=0, concat_axis=0, tiled=True, axis_index_groups=groups)

    def exchange(x):
        return swap(x.reshape(EXPERTS, SLOTS, width)).reshape(rows, width)

    gate_b = jnp.dot(bwd_saved[0], gate_w, preferred_element_type=F32)
    up_b = jnp.dot(bwd_saved[0], up_w, preferred_element_type=F32)
    sig = jax.nn.sigmoid(gate_b)
    act_b = (gate_b * sig * up_b).astype(BF16)
    act_all = swap(jnp.broadcast_to(act_b[None], (len(near[0]),) + act_b.shape), "dp", near)

    cot = exchange(select(bwd_routes, bwd_weights, bwd_grads, True))
    cot_all = swap(split_columns(cot, len(near[0])), "dp", near)

    rows_a = exchange(select(fwd_routes, fwd_weights, fwd_tokens, False))

    dact = lax.dot_general(cot, down_w, contract_last, preferred_element_type=F32)
    dgate = (dact * up_b * sig * (1.0 + gate_b * (1.0 - sig))).astype(BF16)
    dup = (dact * gate_b * sig).astype(BF16)
    row_b = lax.dot_general(dgate, gate_w, contract_last, preferred_element_type=F32)
    row_b = row_b + lax.dot_general(dup, up_w, contract_last, preferred_element_type=F32)
    back_b = exchange(row_b.astype(BF16))

    part = grad_part(cot_all, act_all)
    part = swap(part.reshape(fars, part.shape[0] // fars, part.shape[1]), "dp", far)
    down_grad = jnp.sum(part.astype(F32), axis=0)[None]

    gate_a = jnp.dot(rows_a, gate_w, preferred_element_type=F32)
    up_a = jnp.dot(rows_a, up_w, preferred_element_type=F32)
    act_a = (jax.nn.silu(gate_a) * up_a).astype(BF16)
    row_a = jnp.dot(act_a, down_w, preferred_element_type=F32).astype(BF16)
    back_a = exchange(row_a)

    fwd_out = combine(fwd_routes, fwd_weights, back_a, True)
    input_grad = combine(bwd_routes, bwd_weights, back_b, False)
    return fwd_out, input_grad, down_grad


def solution(mesh):
    in_specs = (P(("ep", "dp"), None),) * 6 + (P("ep", "dp", None),) + (P("ep", None, None),) * 3
    out_specs = (P(("ep", "dp"), None), P(("ep", "dp"), None), P("ep", "dp", None))
    return jax.shard_map(on_device, mesh=mesh, in_specs=in_specs, out_specs=out_specs, check_vma=False)
```

```python
import jax
import jax.numpy as jnp
from jax import lax
from jax.experimental import pallas as pl
from jax.sharding import PartitionSpec as P

EXPERTS = 16
SLOTS = 8
NEAR = 4
BF16, F32 = jnp.bfloat16, jnp.float32


def slot_matrix(routes_t, weights_t):
    picks, tokens = routes_t.shape
    rows = EXPERTS * SLOTS
    row = lax.broadcasted_iota(jnp.int32, (rows, tokens), 0)
    expert, slot = row // SLOTS, row % SLOTS
    member = jnp.zeros((rows, tokens), F32)
    mixing = jnp.zeros((rows, tokens), F32)
    for k in range(picks):
        hit = routes_t[k : k + 1, :] == expert
        member = member + jnp.where(hit, 1.0, 0.0)
        mixing = mixing + jnp.where(hit, weights_t[k : k + 1, :], 0.0)
    earlier = lax.broadcasted_iota(jnp.int32, (tokens, tokens), 0) < lax.broadcasted_iota(
        jnp.int32, (tokens, tokens), 1
    )
    before = jnp.dot(
        member.astype(BF16), jnp.where(earlier, 1.0, 0.0).astype(BF16), preferred_element_type=F32
    )
    chosen = (member > 0.5) & (before.astype(jnp.int32) == slot)
    return jnp.where(chosen, 1.0, 0.0), jnp.where(chosen, mixing, 0.0)


def select_kernel(scaled, routes_ref, weights_ref, x_ref, out_ref):
    chosen, mixing = slot_matrix(routes_ref[...], weights_ref[...])
    scale = jnp.sum(mixing, axis=1, keepdims=True)
    chosen = chosen.astype(BF16)
    for c in range(0, x_ref.shape[1], 256):
        rows = jnp.dot(chosen, x_ref[:, c : c + 256], preferred_element_type=F32)
        if scaled:
            rows = rows * scale
        out_ref[:, c : c + 256] = rows.astype(BF16)


def select(routes, weights, x, scaled):
    import functools

    rows, width = EXPERTS * SLOTS, x.shape[1]
    return pl.pallas_call(
        functools.partial(select_kernel, scaled),
        out_shape=jax.ShapeDtypeStruct((rows, width), BF16),
        cost_estimate=pl.CostEstimate(flops=2 * rows * 16 * width, bytes_accessed=rows * width * 4, transcendentals=0),
        name="select_scaled" if scaled else "select_plain",
    )(routes.T, weights.T, x)


def combine_kernel(weighted, routes_ref, weights_ref, rows_ref, out_ref):
    chosen, mixing = slot_matrix(routes_ref[...], weights_ref[...])
    if weighted:
        high = mixing.astype(BF16)
        rest = mixing - high.astype(F32)
        middle = rest.astype(BF16)
        low = (rest - middle.astype(F32)).astype(BF16)
        parts = [low, middle, high]
    else:
        parts = [chosen.astype(BF16)]
    parts = [p.astype(F32).T.astype(BF16) for p in parts]
    for c in range(0, rows_ref.shape[1], 512):
        rows = rows_ref[:, c : c + 512]
        total = jnp.dot(parts[0], rows, preferred_element_type=F32)
        for p in parts[1:]:
            total = total + jnp.dot(p, rows, preferred_element_type=F32)
        out_ref[:, c : c + 512] = total.astype(BF16)


def combine(routes, weights, rows, weighted):
    import functools

    return pl.pallas_call(
        functools.partial(combine_kernel, weighted),
        out_shape=jax.ShapeDtypeStruct((routes.shape[0], rows.shape[1]), BF16),
        cost_estimate=pl.CostEstimate(flops=10**7, bytes_accessed=rows.size * 2, transcendentals=0),
        name="combine_weighted" if weighted else "combine_plain",
    )(routes.T, weights.T, rows)


def on_device(
    fwd_tokens, fwd_routes, fwd_weights, bwd_grads, bwd_routes, bwd_weights, bwd_saved, w_gate, w_up, w_down
):
    dp = lax.axis_size("dp")
    depth = dp // 2
    me = lax.axis_index("dp")
    upper = lax.shift_right_logical(me, depth.bit_length() - 1) & 1
    width = fwd_tokens.shape[1]
    rows = EXPERTS * SLOTS
    contract_last = (((1,), (1,)), ((), ()))
    contract_rows = (((0,), (0,)), ((), ()))
    gate_w, up_w, down_w = w_gate[0], w_up[0], w_down[0]

    def all_swap(x, axis, groups=None):
        return lax.all_to_all(x, axis, split_axis=0, concat_axis=0, tiled=True, axis_index_groups=groups)

    def exchange(x):
        return all_swap(x.reshape(EXPERTS, SLOTS, width), "ep").reshape(rows, width)

    def piece(x, index, size, axis):
        start = [0] * x.ndim
        start[axis] = index * size
        shape = x.shape[:axis] + (size,) + x.shape[axis + 1 :]
        return lax.dynamic_slice(x, start, shape, allow_negative_indices=False)

    def with_partner(x, bit):
        return lax.ppermute(x, "dp", [(d, d ^ bit) for d in range(dp)])

    cot = exchange(select(bwd_routes, bwd_weights, bwd_grads, True))
    rows_a = exchange(select(fwd_routes, fwd_weights, fwd_tokens, False))

    gate_b = jnp.dot(bwd_saved[0], gate_w, preferred_element_type=F32)
    up_b = jnp.dot(bwd_saved[0], up_w, preferred_element_type=F32)
    sig = jax.nn.sigmoid(gate_b)
    act_b = (gate_b * sig * up_b).astype(BF16)
    act_far = with_partner(act_b, depth)

    half = width // 2
    cot_far = with_partner(piece(cot, 1 - upper, half, 1), depth)
    cot_near = piece(cot, upper, half, 1)
    total = lax.dot_general(cot_near, act_b, contract_rows, preferred_element_type=F32)
    total = total + lax.dot_general(cot_far, act_far, contract_rows, preferred_element_type=F32)

    count, bit = depth, 1
    block = half // depth
    total = total.reshape(count, block, total.shape[1])
    while bit < NEAR:
        mine = lax.shift_right_logical(me, bit.bit_length() - 1) & 1
        pairs = total.reshape(count // 2, 2, block, total.shape[2])
        away = piece(pairs, 1 - mine, 1, 1).squeeze(1).astype(BF16)
        kept = piece(pairs, mine, 1, 1).squeeze(1)
        total = kept + with_partner(away, bit).astype(F32)
        count, bit = count // 2, bit * 2
    groups = [[x * depth + f * NEAR + k for f in range(count)] for x in range(2) for k in range(NEAR)]
    parts = all_swap(total.astype(BF16), "dp", groups)
    down_grad = jnp.sum(parts.astype(F32), axis=0)[None]

    dact = lax.dot_general(cot, down_w, contract_last, preferred_element_type=F32)
    dgate = (dact * up_b * sig * (1.0 + gate_b * (1.0 - sig))).astype(BF16)
    dup = (dact * gate_b * sig).astype(BF16)
    row_b = lax.dot_general(dgate, gate_w, contract_last, preferred_element_type=F32)
    row_b = row_b + lax.dot_general(dup, up_w, contract_last, preferred_element_type=F32)
    back_b = exchange(row_b.astype(BF16))

    gate_a = jnp.dot(rows_a, gate_w, preferred_element_type=F32)
    up_a = jnp.dot(rows_a, up_w, preferred_element_type=F32)
    act_a = (jax.nn.silu(gate_a) * up_a).astype(BF16)
    row_a = jnp.dot(act_a, down_w, preferred_element_type=F32).astype(BF16)
    back_a = exchange(row_a)

    fwd_out = combine(fwd_routes, fwd_weights, back_a, True)
    input_grad = combine(bwd_routes, bwd_weights, back_b, False)
    return fwd_out, input_grad, down_grad


def solution(mesh):
    in_specs = (P(("ep", "dp"), None),) * 6 + (P("ep", "dp", None),) + (P("ep", None, None),) * 3
    out_specs = (P(("ep", "dp"), None), P(("ep", "dp"), None), P("ep", "dp", None))

    return jax.shard_map(on_device, mesh=mesh, in_specs=in_specs, out_specs=out_specs, check_vma=False)
```

```python
import jax
import jax.numpy as jnp
from jax import lax
from jax.experimental import pallas as pl
from jax.sharding import PartitionSpec as P

EXPERTS = 16
SLOTS = 8
BF16, F32 = jnp.bfloat16, jnp.float32


def slot_matrix(routes_t, weights_t):
    picks, tokens = routes_t.shape
    rows = EXPERTS * SLOTS
    row = lax.broadcasted_iota(jnp.int32, (rows, tokens), 0)
    expert, slot = row // SLOTS, row % SLOTS
    member = jnp.zeros((rows, tokens), F32)
    mixing = jnp.zeros((rows, tokens), F32)
    for k in range(picks):
        hit = routes_t[k : k + 1, :] == expert
        member = member + jnp.where(hit, 1.0, 0.0)
        mixing = mixing + jnp.where(hit, weights_t[k : k + 1, :], 0.0)
    earlier = lax.broadcasted_iota(jnp.int32, (tokens, tokens), 0) < lax.broadcasted_iota(
        jnp.int32, (tokens, tokens), 1
    )
    before = jnp.dot(
        member.astype(BF16), jnp.where(earlier, 1.0, 0.0).astype(BF16), preferred_element_type=F32
    )
    chosen = (member > 0.5) & (before.astype(jnp.int32) == slot)
    return jnp.where(chosen, 1.0, 0.0), jnp.where(chosen, mixing, 0.0)


def select_kernel(scaled, routes_ref, weights_ref, x_ref, out_ref):
    chosen, mixing = slot_matrix(routes_ref[...], weights_ref[...])
    scale = jnp.sum(mixing, axis=1, keepdims=True)
    chosen = chosen.astype(BF16)
    for c in range(0, x_ref.shape[1], 256):
        rows = jnp.dot(chosen, x_ref[:, c : c + 256], preferred_element_type=F32)
        if scaled:
            rows = rows * scale
        out_ref[:, c : c + 256] = rows.astype(BF16)


def select(routes, weights, x, scaled):
    import functools

    rows, width = EXPERTS * SLOTS, x.shape[1]
    return pl.pallas_call(
        functools.partial(select_kernel, scaled),
        out_shape=jax.ShapeDtypeStruct((rows, width), BF16),
        cost_estimate=pl.CostEstimate(flops=2 * rows * 16 * width, bytes_accessed=rows * width * 4, transcendentals=0),
        name="select_scaled" if scaled else "select_plain",
    )(routes.T, weights.T, x)


def combine_kernel(weighted, routes_ref, weights_ref, rows_ref, out_ref):
    chosen, mixing = slot_matrix(routes_ref[...], weights_ref[...])
    if weighted:
        high = mixing.astype(BF16)
        rest = mixing - high.astype(F32)
        middle = rest.astype(BF16)
        low = (rest - middle.astype(F32)).astype(BF16)
        parts = [low, middle, high]
    else:
        parts = [chosen.astype(BF16)]
    parts = [p.astype(F32).T.astype(BF16) for p in parts]
    for c in range(0, rows_ref.shape[1], 512):
        rows = rows_ref[:, c : c + 512]
        total = jnp.dot(parts[0], rows, preferred_element_type=F32)
        for p in parts[1:]:
            total = total + jnp.dot(p, rows, preferred_element_type=F32)
        out_ref[:, c : c + 512] = total.astype(BF16)


def combine(routes, weights, rows, weighted):
    import functools

    return pl.pallas_call(
        functools.partial(combine_kernel, weighted),
        out_shape=jax.ShapeDtypeStruct((routes.shape[0], rows.shape[1]), BF16),
        cost_estimate=pl.CostEstimate(flops=10**7, bytes_accessed=rows.size * 2, transcendentals=0),
        name="combine_weighted" if weighted else "combine_plain",
    )(routes.T, weights.T, rows)


def on_device(
    fwd_tokens, fwd_routes, fwd_weights, bwd_grads, bwd_routes, bwd_weights, bwd_saved, w_gate, w_up, w_down
):
    dp = lax.axis_size("dp")
    depth = dp // 2
    me = lax.axis_index("dp")
    upper = lax.shift_right_logical(me, depth.bit_length() - 1) & 1
    width = fwd_tokens.shape[1]
    rows = EXPERTS * SLOTS
    contract_last = (((1,), (1,)), ((), ()))
    contract_rows = (((0,), (0,)), ((), ()))
    gate_w, up_w, down_w = w_gate[0], w_up[0], w_down[0]

    def exchange(x):
        x = x.reshape(EXPERTS, SLOTS, width)
        return lax.all_to_all(x, "ep", split_axis=0, concat_axis=0, tiled=True).reshape(rows, width)

    def piece(x, index, size, axis):
        start = [0] * x.ndim
        start[axis] = index * size
        shape = x.shape[:axis] + (size,) + x.shape[axis + 1 :]
        return lax.dynamic_slice(x, start, shape, allow_negative_indices=False)

    def with_partner(x, bit):
        return lax.ppermute(x, "dp", [(d, d ^ bit) for d in range(dp)])

    cot = exchange(select(bwd_routes, bwd_weights, bwd_grads, True))
    rows_a = exchange(select(fwd_routes, fwd_weights, fwd_tokens, False))

    gate_b = jnp.dot(bwd_saved[0], gate_w, preferred_element_type=F32)
    up_b = jnp.dot(bwd_saved[0], up_w, preferred_element_type=F32)
    sig = jax.nn.sigmoid(gate_b)
    act_b = (gate_b * sig * up_b).astype(BF16)
    act_far = with_partner(act_b, depth)

    half = width // 2
    cot_far = with_partner(piece(cot, 1 - upper, half, 1), depth)
    cot_near = piece(cot, upper, half, 1)
    total = lax.dot_general(cot_near, act_b, contract_rows, preferred_element_type=F32)
    total = total + lax.dot_general(cot_far, act_far, contract_rows, preferred_element_type=F32)

    count, bit = depth, 1
    block = half // depth
    total = total.reshape(count, block, total.shape[1])
    while count > 1:
        mine = lax.shift_right_logical(me, bit.bit_length() - 1) & 1
        pairs = total.reshape(count // 2, 2, block, total.shape[2])
        away = piece(pairs, 1 - mine, 1, 1).squeeze(1).astype(BF16)
        kept = piece(pairs, mine, 1, 1).squeeze(1)
        arrived = with_partner(away, bit)
        total = kept + arrived.astype(F32)
        count, bit = count // 2, bit * 2
    down_grad = total

    dact = lax.dot_general(cot, down_w, contract_last, preferred_element_type=F32)
    dgate = (dact * up_b * sig * (1.0 + gate_b * (1.0 - sig))).astype(BF16)
    dup = (dact * gate_b * sig).astype(BF16)
    row_b = lax.dot_general(dgate, gate_w, contract_last, preferred_element_type=F32)
    row_b = row_b + lax.dot_general(dup, up_w, contract_last, preferred_element_type=F32)
    back_b = exchange(row_b.astype(BF16))

    gate_a = jnp.dot(rows_a, gate_w, preferred_element_type=F32)
    up_a = jnp.dot(rows_a, up_w, preferred_element_type=F32)
    act_a = (jax.nn.silu(gate_a) * up_a).astype(BF16)
    row_a = jnp.dot(act_a, down_w, preferred_element_type=F32).astype(BF16)
    back_a = exchange(row_a)

    fwd_out = combine(fwd_routes, fwd_weights, back_a, True)
    input_grad = combine(bwd_routes, bwd_weights, back_b, False)
    return fwd_out, input_grad, down_grad


def solution(mesh):
    in_specs = (P(("ep", "dp"), None),) * 6 + (P("ep", "dp", None),) + (P("ep", None, None),) * 3
    out_specs = (P(("ep", "dp"), None), P(("ep", "dp"), None), P("ep", "dp", None))

    return jax.shard_map(on_device, mesh=mesh, in_specs=in_specs, out_specs=out_specs, check_vma=False)
```

```python
import jax
import jax.numpy as jnp
from jax import lax
from jax.experimental import pallas as pl
from jax.sharding import PartitionSpec as P

EXPERTS = 16
SLOTS = 8
FAR = 4
BF16, F32 = jnp.bfloat16, jnp.float32


def slot_matrix(routes_t, weights_t):
    picks, tokens = routes_t.shape
    rows = EXPERTS * SLOTS
    row = lax.broadcasted_iota(jnp.int32, (rows, tokens), 0)
    expert, slot = row // SLOTS, row % SLOTS
    member = jnp.zeros((rows, tokens), F32)
    mixing = jnp.zeros((rows, tokens), F32)
    for k in range(picks):
        hit = routes_t[k : k + 1, :] == expert
        member = member + jnp.where(hit, 1.0, 0.0)
        mixing = mixing + jnp.where(hit, weights_t[k : k + 1, :], 0.0)
    earlier = lax.broadcasted_iota(jnp.int32, (tokens, tokens), 0) < lax.broadcasted_iota(
        jnp.int32, (tokens, tokens), 1
    )
    before = jnp.dot(
        member.astype(BF16), jnp.where(earlier, 1.0, 0.0).astype(BF16), preferred_element_type=F32
    )
    chosen = (member > 0.5) & (before.astype(jnp.int32) == slot)
    return jnp.where(chosen, 1.0, 0.0), jnp.where(chosen, mixing, 0.0)


def select_kernel(scaled, routes_ref, weights_ref, x_ref, out_ref):
    chosen, mixing = slot_matrix(routes_ref[...], weights_ref[...])
    scale = jnp.sum(mixing, axis=1, keepdims=True)
    chosen = chosen.astype(BF16)
    for c in range(0, x_ref.shape[1], 256):
        rows = jnp.dot(chosen, x_ref[:, c : c + 256], preferred_element_type=F32)
        if scaled:
            rows = rows * scale
        out_ref[:, c : c + 256] = rows.astype(BF16)


def select(routes, weights, x, scaled):
    import functools

    rows, width = EXPERTS * SLOTS, x.shape[1]
    return pl.pallas_call(
        functools.partial(select_kernel, scaled),
        out_shape=jax.ShapeDtypeStruct((rows, width), BF16),
        cost_estimate=pl.CostEstimate(flops=2 * rows * 16 * width, bytes_accessed=rows * width * 4, transcendentals=0),
        name="select_scaled" if scaled else "select_plain",
    )(routes.T, weights.T, x)


def combine_kernel(weighted, routes_ref, weights_ref, rows_ref, out_ref):
    chosen, mixing = slot_matrix(routes_ref[...], weights_ref[...])
    if weighted:
        high = mixing.astype(BF16)
        rest = mixing - high.astype(F32)
        middle = rest.astype(BF16)
        low = (rest - middle.astype(F32)).astype(BF16)
        parts = [low, middle, high]
    else:
        parts = [chosen.astype(BF16)]
    parts = [p.astype(F32).T.astype(BF16) for p in parts]
    for c in range(0, rows_ref.shape[1], 512):
        rows = rows_ref[:, c : c + 512]
        total = jnp.dot(parts[0], rows, preferred_element_type=F32)
        for p in parts[1:]:
            total = total + jnp.dot(p, rows, preferred_element_type=F32)
        out_ref[:, c : c + 512] = total.astype(BF16)


def combine(routes, weights, rows, weighted):
    import functools

    return pl.pallas_call(
        functools.partial(combine_kernel, weighted),
        out_shape=jax.ShapeDtypeStruct((routes.shape[0], rows.shape[1]), BF16),
        cost_estimate=pl.CostEstimate(flops=10**7, bytes_accessed=rows.size * 2, transcendentals=0),
        name="combine_weighted" if weighted else "combine_plain",
    )(routes.T, weights.T, rows)


def on_device(
    fwd_tokens, fwd_routes, fwd_weights, bwd_grads, bwd_routes, bwd_weights, bwd_saved, w_gate, w_up, w_down
):
    dp = lax.axis_size("dp")
    depth = dp // 2
    me = lax.axis_index("dp")
    upper = lax.shift_right_logical(me, depth.bit_length() - 1) & 1
    width = fwd_tokens.shape[1]
    rows = EXPERTS * SLOTS
    contract_last = (((1,), (1,)), ((), ()))
    contract_rows = (((0,), (0,)), ((), ()))
    gate_w, up_w, down_w = w_gate[0], w_up[0], w_down[0]

    def exchange(x):
        x = x.reshape(EXPERTS, SLOTS, width)
        return lax.all_to_all(x, "ep", split_axis=0, concat_axis=0, tiled=True).reshape(rows, width)

    def piece(x, index, size, axis):
        start = [0] * x.ndim
        start[axis] = index * size
        shape = x.shape[:axis] + (size,) + x.shape[axis + 1 :]
        return lax.dynamic_slice(x, start, shape, allow_negative_indices=False)

    def with_partner(x, bit):
        return lax.ppermute(x, "dp", [(d, d ^ bit) for d in range(dp)])

    cot = exchange(select(bwd_routes, bwd_weights, bwd_grads, True))
    rows_a = exchange(select(fwd_routes, fwd_weights, fwd_tokens, False))

    gate_b = jnp.dot(bwd_saved[0], gate_w, preferred_element_type=F32)
    up_b = jnp.dot(bwd_saved[0], up_w, preferred_element_type=F32)
    sig = jax.nn.sigmoid(gate_b)
    act_b = (gate_b * sig * up_b).astype(BF16)
    act_far = with_partner(act_b, depth)

    half = width // 2
    cot_far = with_partner(piece(cot, 1 - upper, half, 1), depth)
    cot_near = piece(cot, upper, half, 1)
    total = lax.dot_general(cot_near, act_b, contract_rows, preferred_element_type=F32)
    total = total + lax.dot_general(cot_far, act_far, contract_rows, preferred_element_type=F32)

    count, bit = depth, 1
    block = half // depth
    kept, arrived = total.reshape(count, block, total.shape[1]), None

    def share(index, group):
        def part(x):
            x = x.reshape((x.shape[0] // group, group) + x.shape[1:])
            return piece(x, index, 1, 1).squeeze(1)

        mine = part(kept)
        return mine if arrived is None else mine + part(arrived).astype(F32)

    while count > FAR:
        mine = lax.shift_right_logical(me, bit.bit_length() - 1) & 1
        away = share(1 - mine, 2).astype(BF16)
        next_kept = share(mine, 2)
        kept, arrived = next_kept, with_partner(away, bit)
        count, bit = count // 2, bit * 2

    mine = lax.shift_right_logical(me, bit.bit_length() - 1) & (FAR - 1)
    down_grad, shares = None, []
    for step in (2, 1, 3):
        away = share(mine ^ step, FAR).astype(BF16)
        shares.append(with_partner(away, step * bit))
    down_grad = share(mine, FAR)
    for part in shares:
        down_grad = down_grad + part.astype(F32)

    dact = lax.dot_general(cot, down_w, contract_last, preferred_element_type=F32)
    dgate = (dact * up_b * sig * (1.0 + gate_b * (1.0 - sig))).astype(BF16)
    dup = (dact * gate_b * sig).astype(BF16)
    row_b = lax.dot_general(dgate, gate_w, contract_last, preferred_element_type=F32)
    row_b = row_b + lax.dot_general(dup, up_w, contract_last, preferred_element_type=F32)
    back_b = exchange(row_b.astype(BF16))

    gate_a = jnp.dot(rows_a, gate_w, preferred_element_type=F32)
    up_a = jnp.dot(rows_a, up_w, preferred_element_type=F32)
    act_a = (jax.nn.silu(gate_a) * up_a).astype(BF16)
    row_a = jnp.dot(act_a, down_w, preferred_element_type=F32).astype(BF16)
    back_a = exchange(row_a)

    fwd_out = combine(fwd_routes, fwd_weights, back_a, True)
    input_grad = combine(bwd_routes, bwd_weights, back_b, False)
    return fwd_out, input_grad, down_grad


def solution(mesh):
    in_specs = (P(("ep", "dp"), None),) * 6 + (P("ep", "dp", None),) + (P("ep", None, None),) * 3
    out_specs = (P(("ep", "dp"), None), P(("ep", "dp"), None), P("ep", "dp", None))

    return jax.shard_map(on_device, mesh=mesh, in_specs=in_specs, out_specs=out_specs, check_vma=False)
```
